256 devices in a mesh: band: 4 (over x_hi, core), grid: 64 (over x_lo, z, y).
Axes of the slice: x: 4 (x_hi: 2, x_lo: 2; x = x_hi * 2 + x_lo), y: 4, z: 8, core: 2. Of those that a mesh axis runs over, the one named last changes fastest.
Arguments:
- orbitals: float32 [768, 16, 16, 512], P('grid', None, None, 'band'), may hold values from -24 to 24
- potential: float32 [768, 16, 16], P('grid'), may hold values from -3 to -1
- projectors: float32 [256, 8, 13, 256], P('grid'), may hold values from -0.109375 to 0.109375
- atom_planes: int32 [256, 13], P('grid'), may hold values from 0 to 23, as said below
- kb_energy: float32 [8], replicated, may hold values from 1 to 4
Outputs:
- filtered: float32 [768, 16, 16, 512], P('grid', None, None, 'band')
- correlation_gram: float32 [512, 512], P('band')
The draws below stay inside these ranges and needn't reach their ends.
Inputs may be any that keep to these rules, and one draw needn't show every extreme that they name: `atom_planes`: each atom's row holds 13 consecutive plane numbers; the first atom starts at plane 0 and the last atom at plane 12 - 1.
All inputs are finite; a program needn't handle non-finite values.
Results may differ from the reference program's by a relative error of at most 0.0003.
Values sent between devices are 32-bit elements; how exact they have to be, the bound alone decides.
A program may use at most 128 MiB of HBM per device.

```python
import jax
import jax.numpy as jnp
from jax import lax

NORB = 512
CX = 12
NY = 16
NZ = 16
ATOM_DEV = 4
NPJ = 8
NBLK = 13
DEGREE = 4
NX = 768
NATOM = 256
CELLS = 196608


def draw_atom_planes(key, part):
    offsets = jax.random.randint(key, (NATOM,), 0, CX, dtype=jnp.int32)
    offsets = offsets.at[0].set(0).at[NATOM - 1].set(CX - 1)
    return offsets[:, None] + jnp.arange(NBLK, dtype=jnp.int32)[None, :]


def block_scale(own_key, extent, shards, least, top_value):
    factor_of, own = 1.0, jax.random.fold_in(own_key, 6)
    for dim, parts in shards:
        draws = jnp.exp(jax.random.uniform(jax.random.fold_in(own, dim), (parts,), jnp.float32, least / len(shards), top_value / len(shards)))
        factor_of = factor_of * jnp.repeat(draws, extent[dim] // parts).reshape([-1 if axis == dim else 1 for axis in range(len(extent))])
    return factor_of


def noise(rng, dims, spread, limit, cuts=(), kind=jnp.bfloat16):
    array = spread * jax.random.normal(rng, dims, jnp.float32)
    if cuts:
        array = array * block_scale(rng, dims, cuts, -0.22, 0.18)
    return jnp.clip(array, -limit, limit).astype(kind)


def setup_inputs(seed: int = 0) -> dict:
    streams_of = jax.random.split(jax.random.key(seed), 6)
    orbitals = noise(streams_of[0], (NX, NY, NZ, NORB), 4.0, 24.0, ((0, 64), (3, 4)), jnp.float32)
    potential = jnp.clip(-3.0 + 2.0 * jax.random.uniform(streams_of[1], (NX, NY, NZ), jnp.float32) ** block_scale(streams_of[1], (NX, NY, NZ), ((0, 64),), -0.2, 0.2), -3.0, -1.0)
    projectors = noise(streams_of[2], (NATOM, NPJ, NBLK, NY * NZ), (NBLK * NY * NZ) ** -0.5, 0.109375, ((0, 64),), jnp.float32)
    atom_planes = draw_atom_planes(jax.random.fold_in(streams_of[5], 71), 0)
    kb_energy = jnp.clip(jax.random.uniform(streams_of[4], (NPJ,), jnp.float32, 1.0, 4.0), 1.0, 4.0)
    return dict(orbitals=orbitals, potential=potential, projectors=projectors, atom_planes=atom_planes, kb_energy=kb_energy)


WEIGHTS = (-5369.0 / 1800.0, 12.0 / 7.0, -15.0 / 56.0, 10.0 / 189.0, -1.0 / 112.0, 2.0 / 1925.0, -1.0 / 16632.0)
LOWER = -4.0
CUTOFF = 1.0
UPPER = 16.0
PRECISE = lax.Precision.HIGHEST


def filter_terms(degree):
    half_span = (UPPER - CUTOFF) / 2.0
    middle = (UPPER + CUTOFF) / 2.0
    sigma_now = half_span / (LOWER - middle)
    sigma_first = sigma_now
    scales = [sigma_now / half_span]
    recall = [0.0]
    for level in range(1, degree):
        sigma_next = 1.0 / (2.0 / sigma_first - sigma_now)
        scales.append(2.0 * sigma_next / half_span)
        recall.append(sigma_now * sigma_next)
        sigma_now = sigma_next
    return middle, scales, recall


def second_roll(values, along):
    summed = WEIGHTS[0] * values
    for reach in range(1, 7):
        summed = summed + WEIGHTS[reach] * (jnp.roll(values, reach, along) + jnp.roll(values, -reach, along))
    return summed


def nonlocal_term(values, projectors, atom_planes, kb_energy):
    offsets = (jnp.arange(NATOM, dtype=jnp.int32) // ATOM_DEV) * CX - 6

    def add_atom(accum, atom_data):
        chi_rows, rows_here, offset = atom_data
        plane_ids = ((offset + rows_here) % NX).astype(jnp.int32)
        gathered = values[plane_ids].reshape(-1, NORB)
        chi_flat = chi_rows.reshape(NPJ, -1)
        correlation = jnp.dot(chi_flat, gathered, precision=PRECISE) * kb_energy[:, None]
        contrib = lax.dot_general(chi_flat, correlation, (((0,), (0,)), ((), ())), precision=PRECISE)
        return accum.at[plane_ids].add(contrib.reshape(NBLK, NY, NZ, NORB)), None

    accum, unused = lax.scan(add_atom, jnp.zeros_like(values), (projectors, atom_planes, offsets))
    return accum


def hamiltonian(values, potential, projectors, atom_planes, kb_energy):
    lap = second_roll(values, 0) + second_roll(values, 1) + second_roll(values, 2)
    local_part = -0.5 * lap + potential[..., None] * values
    return local_part + nonlocal_term(values, projectors, atom_planes, kb_energy)


def reference(orbitals, potential, projectors, atom_planes, kb_energy):
    middle, scales, recall = filter_terms(DEGREE)
    previous = orbitals
    current = orbitals
    for level in range(DEGREE):
        applied = hamiltonian(current, potential, projectors, atom_planes, kb_energy)
        result = scales[level] * (applied - middle * current)
        if level > 0:
            result = result - recall[level] * previous
        previous = current
        current = result
    flattened = current.reshape(-1, NORB)
    correlation_gram = lax.dot_general(flattened, flattened, (((0,), (0,)), ((), ())), precision=PRECISE) * (1.0 / CELLS)
    return current, correlation_gram
```

```python
import functools

import jax
import jax.numpy as jnp
import ml_dtypes
import numpy as np
from jax import lax
from jax.experimental import pallas as pl
from jax.experimental.pallas import tpu as pltpu
from jax.sharding import PartitionSpec as P

DEGREE = 4
WEIGHTS = (
    -5369.0 / 1800.0,
    12.0 / 7.0,
    -15.0 / 56.0,
    10.0 / 189.0,
    -1.0 / 112.0,
    2.0 / 1925.0,
    -1.0 / 16632.0,
)
LOWER = -4.0
CUTOFF = 1.0
UPPER = 16.0
REACH = 6
CHUNKS = 4
YPEERS = 4
MESH = pl.DeviceIdType.MESH
F32 = jnp.float32
BF16 = jnp.bfloat16


def filter_terms(degree):
    half_span = (UPPER - CUTOFF) / 2.0
    middle = (UPPER + CUTOFF) / 2.0
    sigma_now = half_span / (LOWER - middle)
    sigma_first = sigma_now
    scales = [sigma_now / half_span]
    recall = [0.0]
    for level in range(1, degree):
        sigma_next = 1.0 / (2.0 / sigma_first - sigma_now)
        scales.append(2.0 * sigma_next / half_span)
        recall.append(sigma_now * sigma_next)
        sigma_now = sigma_next
    return (middle, scales, recall)


def plane_matrix(ny, nz):
    cells = ny * nz
    matrix = np.zeros((cells, cells))
    for y in range(ny):
        for z in range(nz):
            for reach in range(1, REACH + 1):
                for by in (reach, -reach):
                    matrix[y * nz + z, ((y + by) % ny) * nz + z] += -0.5 * WEIGHTS[reach]
                    matrix[y * nz + z, y * nz + (z + by) % nz] += -0.5 * WEIGHTS[reach]
    high = matrix.astype(ml_dtypes.bfloat16)
    low = (matrix - high.astype(np.float64)).astype(ml_dtypes.bfloat16)
    return np.concatenate([high, low], axis=0)


def split(value):
    high = value.astype(BF16)
    return high, (value - high.astype(F32)).astype(BF16)


def dot(a, b):
    return jnp.dot(a, b, preferred_element_type=F32)


def place_body(planes, projectors, placed):
    placed[...] = jnp.zeros_like(placed)
    atoms, count, blocks, _ = projectors.shape
    for atom in range(atoms):
        for block in range(blocks):
            placed[planes[atom, block], pl.ds(atom * count, count), :] = projectors[atom, :, block, :]


def main_body(
    cells,
    orb, pot_t, wyz, pown, energy,
    filt, gram,
    ys, halo_lo, halo_hi, diag, local, rim_lo, rim_hi, pstack, qstack,
    cpart, crecv, cown, cnear,
    fb, fc, fd, gacc, xsend, xrecv, gblk, ry, b1, rz, g1, gfull,
    hs, hr, rs_, rr_, ps_, pr_, cs_, cr_, fs_, fr_, xs_, xr_, ys_, yr_, zs_, zr_, as_, ar_, bs_, br_,
):
    slab, rows = orb.shape[0], orb.shape[1]
    step_rows = rows // CHUNKS
    band = lax.axis_index("band")
    grid = lax.axis_index("grid")
    domains = lax.axis_size("grid")
    right = lax.rem(grid + 1, domains)
    left = lax.rem(grid + domains - 1, domains)
    x_hi = band // 2
    partner = band + 1 - 2 * lax.rem(band, 2)
    opposite = lax.rem(band + 2, 4)
    diagonal = lax.rem(partner + 2, 4)
    y_here = lax.rem(grid, YPEERS)
    y_base = grid - y_here
    zx_here = grid // YPEERS
    zx_count = domains // YPEERS
    part_rows = b1.shape[0] // zx_count
    y_peers = [lax.rem(y_here + i, YPEERS) for i in range(1, YPEERS)]
    zx_peers = [lax.rem(zx_here + i, zx_count) for i in range(1, zx_count)]
    middle, scales, recall = filter_terms(DEGREE)
    pending = []

    def remote(src, dst, ssem, rsem, b, g):
        return pltpu.make_async_remote_copy(
            src_ref=src, dst_ref=dst, send_sem=ssem, recv_sem=rsem,
            device_id=(b, g), device_id_type=MESH,
        )

    def start(*copies):
        for copy in copies:
            copy.start()
            pending.append(copy)
        return copies

    barrier = pltpu.get_barrier_semaphore()
    greeted = [(band, left), (band, right), (partner, grid), (opposite, grid), (diagonal, grid)]
    greeted += [(band, y_base + q) for q in y_peers]
    greeted += [(band, m * YPEERS + y_here) for m in zx_peers]
    for b, g in greeted:
        pl.semaphore_signal(barrier, inc=1, device_id=(b, g), device_id_type=MESH)
    for p in range(slab):
        diag[p] = jnp.broadcast_to(
            pot_t[:, p : p + 1] + (-1.5 * WEIGHTS[0] - middle), (rows, orb.shape[2])
        )
    pl.semaphore_wait(barrier, len(greeted))

    def source(level):
        return orb if level == 0 else ys.at[level - 1]

    def halo(level, r):
        cur = source(level)
        at = pl.ds(r * step_rows, step_rows)
        return (
            remote(cur.at[pl.ds(slab - REACH, REACH), at], halo_lo.at[level, :, at],
                   hs.at[level, r, 0], hr.at[level, r, 0], band, right),
            remote(cur.at[pl.ds(0, REACH), at], halo_hi.at[level, :, at],
                   hs.at[level, r, 1], hr.at[level, r, 1], band, left),
        )

    extent = pown.shape[0]
    rims = start(
        remote(pown.at[pl.ds(extent - REACH, REACH)], rim_lo, rs_.at[0], rr_.at[0], band, right),
        remote(pown.at[pl.ds(0, REACH)], rim_hi, rs_.at[1], rr_.at[1], band, left),
    )
    sent = {}
    for r in range(2):
        sent[0, r] = start(*halo(0, r))
    for copy in rims:
        copy.wait_recv()

    def stack_map(low):
        def step(p, carry):
            rim = rim_lo[p] if low else rim_hi[p]
            at = p if low else p + REACH
            both = jnp.concatenate([pown[at + REACH], rim], axis=0)
            high, rest = split(both)
            pstack[at] = jnp.concatenate([high, rest], axis=0)
            high = high.astype(F32)
            rest = both - high
            turned = jnp.concatenate([high, high, rest, jnp.zeros_like(rest)], axis=0)
            qstack[at] = jnp.transpose(turned).astype(BF16)
            return carry
        lax.fori_loop(0, REACH, step, 0)

    stack_map(True)
    stack_map(False)

    def plane_products(cur, first):
        def step(p, total):
            high, rest = split(cur[p])
            pair = jnp.concatenate([high, rest], axis=1)
            lanes = high.shape[1]
            o = dot(wyz[...], pair)
            local[p] = o[:rows, :lanes] + o[:rows, lanes:] + o[rows:, :lanes]
            q = dot(pstack[p], pair)
            half = q.shape[0] // 2
            return total + (q[:half, :lanes] + q[:half, lanes:] + q[half:, :lanes])
        return lax.fori_loop(
            first, first + REACH, step, jnp.zeros((pstack.shape[1] // 2, orb.shape[2]), F32)
        )

    def spread_on(first, coeff):
        high = coeff.astype(BF16).astype(F32)
        rest = coeff - high
        stacked = jnp.concatenate([high, rest, high, jnp.zeros_like(rest)], axis=0).astype(BF16)

        def step(p, carry):
            local[p] = local[p] + dot(qstack[p], stacked)
            return carry
        lax.fori_loop(first, first + REACH, step, 0)

    def finish(level, r, target, copies):
        for copy in copies:
            copy.wait_recv()
        cur = source(level)
        prev = None if level == 0 else source(level - 1)
        scale = scales[level]
        taps = [-0.5 * scale * w for w in WEIGHTS]

        def step(i, carry):
            at = pl.ds(pl.multiple_of(r * step_rows + i * 8, 8), 8)
            line = [halo_lo[level, j, at] for j in range(REACH)]
            line += [cur[j, at] for j in range(slab)]
            line += [halo_hi[level, j, at] for j in range(REACH)]
            for j in range(slab):
                here = j + REACH
                value = scale * (local[j, at] + diag[j, at] * line[here])
                for reach in range(1, REACH + 1):
                    value = value + taps[reach] * (line[here - reach] + line[here + reach])
                if prev is not None:
                    value = value - recall[level] * prev[j, at]
                target[j, at] = value
            return carry
        lax.fori_loop(0, step_rows // 8, step, 0)

    width = energy.shape[0]
    shared = []
    for level in range(DEGREE):
        cur = source(level)
        low = plane_products(cur, 0)
        high = plane_products(cur, REACH)
        cpart[level, 0] = low[width:]
        cpart[level, 1] = high[width:]
        parts = start(
            remote(cpart.at[level, 1], crecv.at[level, 0], ps_.at[level, 0], pr_.at[level, 0], band, right),
            remote(cpart.at[level, 0], crecv.at[level, 1], ps_.at[level, 1], pr_.at[level, 1], band, left),
        )
        sent[level, 2] = start(*halo(level, 2))
        for copy in parts:
            copy.wait_recv()
        own = (low[:width] + high[:width] + crecv[level, 0] + crecv[level, 1]) * energy[...]
        cown[level] = own
        nears = start(
            remote(cown.at[level], cnear.at[level, 0], cs_.at[level, 0], cr_.at[level, 0], band, right),
            remote(cown.at[level], cnear.at[level, 1], cs_.at[level, 1], cr_.at[level, 1], band, left),
        )
        sent[level, 3] = start(*halo(level, 3))
        for copy in nears:
            copy.wait_recv()
        spread_on(0, jnp.concatenate([own, cnear[level, 0]], axis=0))
        spread_on(REACH, jnp.concatenate([own, cnear[level, 1]], axis=0))
        last = level == DEGREE - 1
        target = filt if last else ys.at[level]
        for r in range(CHUNKS):
            finish(level, r, target, sent[level, r])
            at = pl.ds(r * step_rows, step_rows)
            if not last:
                if r < 2:
                    sent[level + 1, r] = start(*halo(level + 1, r))
                continue
            shared.append(start(
                remote(filt.at[pl.ds(REACH * (1 - x_hi), REACH), at], fc.at[:, at],
                       fs_.at[r, 0], fr_.at[r, 0], opposite, grid),
                remote(filt.at[:, at], fb.at[:, at], fs_.at[r, 1], fr_.at[r, 1], partner, grid),
            ))

    forwarded = []
    for r in range(CHUNKS):
        at = pl.ds(r * step_rows, step_rows)
        shared[r][0].wait_recv()
        forwarded += start(
            remote(fc.at[:, at], fd.at[:, at], fs_.at[r, 2], fr_.at[r, 2], partner, grid)
        )
        shared[r][1].wait_recv()

    def gram_step(mine, other):
        a_high, a_rest = split(jnp.transpose(mine))
        b_high, b_rest = split(other)
        both = jnp.concatenate([a_high, a_rest], axis=0)
        first = dot(both, b_high)
        lanes = a_high.shape[0]
        return first[:lanes] + first[lanes:] + dot(a_high, b_rest)

    gacc[...] = jnp.zeros_like(gacc)

    def own_step(p, carry):
        mine = filt[p]
        gacc[0] = gacc[0] + gram_step(mine, jnp.concatenate([mine, fb[p]], axis=1))
        return carry
    lax.fori_loop(0, slab, own_step, 0)
    for copy in forwarded:
        copy.wait_recv()

    def cross_step(p, carry):
        mine = filt[p + REACH * x_hi]
        gacc[1] = gacc[1] + gram_step(mine, jnp.concatenate([fc[p], fd[p]], axis=1))
        return carry
    lax.fori_loop(0, REACH, cross_step, 0)

    lanes = orb.shape[2]
    xsend[0] = jnp.transpose(gacc[1, :, :lanes])
    xsend[1] = jnp.transpose(gacc[1, :, lanes:])
    crossed = start(
        remote(xsend.at[0], xrecv.at[0], xs_.at[0], xr_.at[0], opposite, grid),
        remote(xsend.at[1], xrecv.at[1], xs_.at[1], xr_.at[1], diagonal, grid),
    )
    gblk[0] = gacc[0, :, :lanes]
    gblk[1] = gacc[0, :, lanes:]
    for copy in crossed:
        copy.wait_recv()
    gblk[2] = gacc[1, :, :lanes] + xrecv[0]
    gblk[3] = gacc[1, :, lanes:] + xrecv[1]

    for i, q in enumerate(y_peers):
        start(remote(gblk.at[q], ry.at[y_here], ys_.at[i], yr_.at[y_here], band, y_base + q))
    total = gblk[y_here]
    for i, q in enumerate(y_peers):
        remote(ry.at[q], ry.at[q], ys_.at[i], yr_.at[q], band, y_base + q).wait_recv()
        total = total + ry[q]
    b1[...] = total

    def piece(ref, n):
        return ref.at[pl.ds(pl.multiple_of(n * part_rows, 8), part_rows)]

    for i, m in enumerate(zx_peers):
        start(remote(piece(b1, m), rz.at[zx_here], zs_.at[i], zr_.at[zx_here],
                     band, m * YPEERS + y_here))
    total = b1[pl.ds(pl.multiple_of(zx_here * part_rows, 8), part_rows)]
    for i, m in enumerate(zx_peers):
        remote(rz.at[m], rz.at[m], zs_.at[i], zr_.at[m], band, m * YPEERS + y_here).wait_recv()
        total = total + rz[m]
    g1[pl.ds(pl.multiple_of(zx_here * part_rows, 8), part_rows)] = total * (1.0 / cells)
    for i, m in enumerate(zx_peers):
        start(remote(piece(g1, zx_here), piece(g1, zx_here), as_.at[i], ar_.at[zx_here],
                     band, m * YPEERS + y_here))
    for i, m in enumerate(zx_peers):
        remote(piece(g1, m), piece(g1, m), as_.at[i], ar_.at[m],
               band, m * YPEERS + y_here).wait_recv()
    for i, q in enumerate(y_peers):
        start(remote(g1, gfull.at[y_here], bs_.at[i], br_.at[y_here], band, y_base + q))
    gfull[y_here] = g1[...]
    for i, q in enumerate(y_peers):
        remote(gfull.at[q], gfull.at[q], bs_.at[i], br_.at[q], band, y_base + q).wait_recv()
    for c in range(4):
        block = 2 * lax.rem(x_hi + c // 2, 2) + lax.rem(lax.rem(band, 2) + c % 2, 2)
        gram[:, c * lanes : (c + 1) * lanes] = gfull[block]
    for copy in pending:
        copy.wait_send()


def shards(orbitals, potential, projectors, atom_planes, kb_energy):
    slab, ny, nz, lanes = orbitals.shape
    rows = ny * nz
    domains = lax.axis_size("grid")
    atoms, count, blocks, _ = projectors.shape
    width = atoms * count
    extent = slab + 2 * REACH
    vmem = pl.BlockSpec(memory_space=pltpu.VMEM)
    placed = pl.pallas_call(
        place_body,
        out_shape=jax.ShapeDtypeStruct((extent, width, rows), F32),
        in_specs=[pl.BlockSpec(memory_space=pltpu.SMEM), vmem],
        out_specs=vmem,
        name="place_projectors",
    )(atom_planes, projectors)
    energy = jnp.broadcast_to(jnp.tile(kb_energy, atoms)[:, None], (width, lanes))
    pot_t = jnp.transpose(potential.reshape(slab, rows))
    zx_count = domains // YPEERS
    dma = pltpu.SemaphoreType.DMA
    big = (slab, rows, lanes)
    rim = (REACH, rows, lanes)
    small = (width, lanes)
    square = (lanes, lanes)
    scratch = [
        pltpu.VMEM((DEGREE - 1, *big), F32),
        pltpu.VMEM((DEGREE, *rim), F32),
        pltpu.VMEM((DEGREE, *rim), F32),
        pltpu.VMEM(big, F32),
        pltpu.VMEM(big, F32),
        pltpu.VMEM((REACH, width, rows), F32),
        pltpu.VMEM((REACH, width, rows), F32),
        pltpu.VMEM((slab, 4 * width, rows), BF16),
        pltpu.VMEM((slab, rows, 8 * width), BF16),
        pltpu.VMEM((DEGREE, 2, *small), F32),
        pltpu.VMEM((DEGREE, 2, *small), F32),
        pltpu.VMEM((DEGREE, *small), F32),
        pltpu.VMEM((DEGREE, 2, *small), F32),
        pltpu.VMEM(big, F32),
        pltpu.VMEM(rim, F32),
        pltpu.VMEM(rim, F32),
        pltpu.VMEM((2, lanes, 2 * lanes), F32),
        pltpu.VMEM((2, *square), F32),
        pltpu.VMEM((2, *square), F32),
        pltpu.VMEM((4, *square), F32),
        pltpu.VMEM((YPEERS, *square), F32),
        pltpu.VMEM(square, F32),
        pltpu.VMEM((zx_count, lanes // zx_count, lanes), F32),
        pltpu.VMEM(square, F32),
        pltpu.VMEM((YPEERS, *square), F32),
        dma((DEGREE, CHUNKS, 2)), dma((DEGREE, CHUNKS, 2)),
        dma((2,)), dma((2,)),
        dma((DEGREE, 2)), dma((DEGREE, 2)),
        dma((DEGREE, 2)), dma((DEGREE, 2)),
        dma((CHUNKS, 3)), dma((CHUNKS, 3)),
        dma((2,)), dma((2,)),
        dma((YPEERS,)), dma((YPEERS,)),
        dma((zx_count,)), dma((zx_count,)),
        dma((zx_count,)), dma((zx_count,)),
        dma((YPEERS,)), dma((YPEERS,)),
    ]
    filtered, gram = pl.pallas_call(
        functools.partial(main_body, slab * rows * domains),
        out_shape=(
            jax.ShapeDtypeStruct(big, F32),
            jax.ShapeDtypeStruct((lanes, 4 * lanes), F32),
        ),
        in_specs=[vmem] * 5,
        out_specs=(vmem, vmem),
        scratch_shapes=scratch,
        compiler_params=pltpu.CompilerParams(
            collective_id=0, has_side_effects=True, vmem_limit_bytes=56 << 20
        ),
        name="filter_and_gram",
    )(orbitals.reshape(big), pot_t, jnp.asarray(plane_matrix(ny, nz)), placed, energy)
    return (filtered.reshape(orbitals.shape), gram)


def solution(mesh):
    return jax.shard_map(
        shards,
        mesh=mesh,
        in_specs=(
            P("grid", None, None, "band"),
            P("grid", None, None),
            P("grid", None, None, None),
            P("grid", None),
            P(),
        ),
        out_specs=(P("grid", None, None, "band"), P("band", None)),
        check_vma=False,
    )
```
